512 devices in a mesh: dp: 8 (over z_lo, core), ctx: 64 (over z_hi, y, x).
Axes of the slice: x: 4, y: 8, z: 8 (z_hi: 2, z_lo: 4; z = z_hi * 4 + z_lo), core: 2. Of those that a mesh axis runs over, the one named last changes fastest.
Arguments:
- queries: bfloat16 [32768, 4096], P(('dp', 'ctx')), parts along dimension 0, as said below
- keys: bfloat16 [32768, 512], P(('dp', 'ctx')), parts along dimension 0, as said below
- values: bfloat16 [32768, 512], P(('dp', 'ctx')), parts along dimension 0, may hold values from -6 to 6
Outputs:
- attended: bfloat16 [32768, 4096], P(('dp', 'ctx')), parts along dimension 0
The draws below stay inside these ranges and needn't reach their ends.
There are 8 independent parts, one for each index of `dp`. The reference program is written for one: setup_inputs(seed, part) draws one part's arguments, and reference() takes and returns one part's arrays. A program takes and returns all parts, laid end to end along the dimension named above; each array names one. Nothing has to cross between parts.
Inputs may be any that keep to these rules, and one draw needn't show every extreme that they name: `queries`: entries lie between -310 / sqrt(128) and 310 / sqrt(128). `keys`: entries lie between -6 and 6.
All inputs are finite; a program needn't handle non-finite values.
Results may differ from the reference program's by a relative error of at most 0.0035.
Values may be sent and summed in bfloat16 or wider, within the bound.
No kernel may reach another device: no remote copies, remote signals or barrier semaphores. Data moves between devices by JAX's collectives and lax.ppermute only.
A program may use at most 128 MiB of HBM per device.

```python
import math
import jax
import jax.numpy as jnp
from jax import lax

QH = 32
KVH = 4
HD = 128
TOK_DEV = 64
SEQ = 4096
N_CTX = 64


def draw_queries(key, part):
    drawn = 3.0 * jax.random.normal(jax.random.fold_in(key, 1), (SEQ, QH * HD), jnp.float32)
    drawn = jnp.clip(drawn, -18.0, 18.0)
    return drawn.astype(jnp.bfloat16)


def draw_keys(key, part):
    drawn = jax.random.normal(jax.random.fold_in(key, 2), (SEQ, KVH * HD), jnp.float32)
    drawn = jnp.clip(drawn, -6.0, 6.0)
    return drawn.astype(jnp.bfloat16)


def steps_of(stream_key, extent, cuts, smallest, largest):
    loudness = 1.0
    for axis_at, parts in cuts:
        steps = jax.random.uniform(jax.random.fold_in(jax.random.fold_in(stream_key, 6), axis_at), (parts,), jnp.float32, smallest / len(cuts), largest / len(cuts))
        loudness = loudness * jnp.repeat(jnp.exp(steps), extent[axis_at] // parts).reshape((-1,) + (1,) * (len(extent) - 1 - axis_at))
    return loudness


def scatter_about(rng, shape, scale, bound, cuts=(), kind=jnp.bfloat16):
    entries = jax.random.normal(rng, shape, jnp.float32) * scale
    if len(cuts) > 0:
        entries = steps_of(rng, shape, cuts, -0.22, 0.18) * entries
    return jnp.clip(entries, min=-bound, max=bound).astype(kind)


def setup_inputs(seed: int = 0, part: int = 0) -> dict:
    seeds = jax.random.split(jax.random.key(seed), 4)
    part_keys = jax.random.split(jax.random.fold_in(seeds[3], part), 4)
    queries = draw_queries(jax.random.fold_in(jax.random.fold_in(seeds[3], part), 71), part)
    keys = draw_keys(jax.random.fold_in(jax.random.fold_in(seeds[3], part), 71), part)
    values = scatter_about(part_keys[2], (SEQ, KVH * HD), 1.0, 6.0, ((0, 64),))
    return {"queries": queries, "keys": keys, "values": values}


def reference(queries, keys, values):
    seq_len = queries.shape[0]
    group_size = QH // KVH
    inverse_root = 1.0 / math.sqrt(HD)
    key_heads = keys.astype(jnp.float32).reshape(seq_len, KVH, HD)
    value_heads = values.astype(jnp.float32).reshape(seq_len, KVH, HD)
    query_blocks = queries.astype(jnp.float32).reshape(N_CTX, TOK_DEV, KVH, group_size, HD)
    offsets = (jnp.arange(N_CTX) * TOK_DEV).astype(jnp.int32)
    key_pos = jnp.arange(seq_len).astype(jnp.int32)

    def attend_block(inputs):
        query_block, offset = inputs
        scores = jnp.einsum('tkgd,skd->kgts', query_block, key_heads) * inverse_root
        query_pos = offset + jnp.arange(TOK_DEV).astype(jnp.int32)
        scores = jnp.where(key_pos[None, :] <= query_pos[:, None], scores, -jnp.inf)
        peak = scores.max(-1, keepdims=True)
        weights = jnp.exp(scores - peak)
        denominator = weights.sum(-1)
        rounded = lax.optimization_barrier(weights.astype(jnp.bfloat16)).astype(jnp.float32)
        mixed_values = jnp.einsum('kgts,skd->tkgd', rounded, value_heads)
        return mixed_values / jnp.transpose(denominator, (2, 0, 1))[..., None]
    finished = lax.map(attend_block, (query_blocks, offsets))
    return finished.reshape(seq_len, QH * HD).astype(jnp.bfloat16)
```

```python
import functools
import math

import jax
import jax.numpy as jnp
from jax import lax
from jax.experimental import pallas as pl
from jax.experimental.pallas import tpu as pltpu
from jax.sharding import PartitionSpec as P

QH = 32
KVH = 4
HD = 128
GROUP = QH // KVH
NZ, NY, NX = 2, 8, 4
ROWS = 256
SCALE = math.log2(math.e) / math.sqrt(HD)
NEG = -1e30
QK = (((1,), (1,)), ((), ()))
UNROLL = 4


def index(z, y, x):
    return z * (NY * NX) + y * NX + x


X_GROUPS = [[index(z, y, x) for x in range(NX)] for z in range(NZ) for y in range(NY)]
Z_GROUPS = [[index(z, y, x) for z in range(NZ)] for y in range(NY) for x in range(NX)]


def ring(step):
    return [
        (index(z, y, x), index(z, (y + step) % NY, x))
        for z in range(NZ)
        for y in range(NY)
        for x in range(NX)
    ]


def columns(head):
    return pl.ds(pl.multiple_of(head * HD, HD), HD)


def lane_sums(weights):
    total = weights[:, :HD]
    for at in range(HD, weights.shape[1], HD):
        total = total + weights[:, at : at + HD]
    return total


def own_kernel(place, x_ref, kv_ref, acc_ref, max_ref, sum_ref):
    def head(j, carry):
        cols = columns(j)
        scores = lax.dot_general(
            x_ref[:, cols], kv_ref[:, :HD], QK, preferred_element_type=jnp.float32
        )
        row = lax.broadcasted_iota(jnp.int32, scores.shape, 0)
        col = lax.broadcasted_iota(jnp.int32, scores.shape, 1)
        scores = jnp.where(col <= row + place[0] * ROWS, scores, NEG)
        peak = jnp.max(scores, axis=1, keepdims=True) * SCALE
        weights = jnp.exp2(scores * SCALE - peak)
        sum_ref[:, cols] = lane_sums(weights)
        acc_ref[:, cols] = jnp.dot(
            weights.astype(jnp.bfloat16),
            kv_ref[:, HD:],
            preferred_element_type=jnp.float32,
        )
        max_ref[:, cols] = jnp.broadcast_to(peak, (ROWS, HD))
        return carry

    lax.fori_loop(0, GROUP, head, 0, unroll=UNROLL)


def absorb(n, x_ref, kv_ref, acc_in, max_in, sum_in, acc_ref, max_ref, sum_ref):
    def head(j, carry):
        cols = columns(j)
        scores = lax.dot_general(
            x_ref[:, cols], kv_ref[:n, :HD], QK, preferred_element_type=jnp.float32
        )
        old = max_in[:, cols]
        peak = jnp.maximum(old, jnp.max(scores, axis=1, keepdims=True) * SCALE)
        keep = jnp.exp2(old - peak)
        weights = jnp.exp2(scores * SCALE - jnp.tile(peak, (1, n // HD)))
        sum_ref[:, cols] = sum_in[:, cols] * keep + lane_sums(weights)
        acc_ref[:, cols] = acc_in[:, cols] * keep + jnp.dot(
            weights.astype(jnp.bfloat16),
            kv_ref[:n, HD:],
            preferred_element_type=jnp.float32,
        )
        max_ref[:, cols] = peak
        return carry

    lax.fori_loop(0, GROUP, head, 0, unroll=UNROLL)


def absorb_if_needed(shift, place, x_ref, kv_ref, ins, outs):
    z, y = place[0], place[1]
    source = lax.rem(y - shift + NY, NY)
    before = source < y

    @pl.when(jnp.logical_and(z == 1, before))
    def _():
        absorb(2 * ROWS, x_ref, kv_ref, *ins, *outs)

    @pl.when(jnp.logical_and(z == 1, jnp.logical_not(before)))
    def _():
        absorb(ROWS, x_ref, kv_ref, *ins, *outs)

    @pl.when(jnp.logical_and(z == 0, before))
    def _():
        absorb(ROWS, x_ref, kv_ref, *ins, *outs)


def more_kernel(shift, place, x_ref, kv_ref, a_in, m_in, s_in, a_out, m_out, s_out):
    absorb_if_needed(
        shift, place, x_ref, kv_ref, (a_in, m_in, s_in), (a_out, m_out, s_out)
    )


def last_kernel(
    shift, place, x_ref, kv_ref, a_in, m_in, s_in, o_ref, a_out, m_out, s_out
):
    absorb_if_needed(
        shift, place, x_ref, kv_ref, (a_in, m_in, s_in), (a_out, m_out, s_out)
    )

    def head(j, carry):
        cols = columns(j)
        total = jnp.sum(s_out[:, cols], axis=1, keepdims=True)
        o_ref[:, cols] = (a_out[:, cols] / total).astype(jnp.bfloat16)
        return carry

    lax.fori_loop(0, GROUP, head, 0, unroll=UNROLL)


VMEM = pl.BlockSpec(memory_space=pltpu.VMEM)
SMEM = pl.BlockSpec(memory_space=pltpu.SMEM)
STATE = [jax.ShapeDtypeStruct((ROWS, GROUP * HD), jnp.float32)] * 3
PARAMS = pltpu.CompilerParams(vmem_limit_bytes=24 << 20)
COST = pl.CostEstimate(
    flops=4 * ROWS * GROUP * 2 * ROWS * HD,
    bytes_accessed=8 << 20,
    transcendentals=ROWS * GROUP * 2 * ROWS,
)


def own_block(place, x, kv):
    return pl.pallas_call(
        own_kernel,
        out_shape=STATE,
        in_specs=[SMEM, VMEM, VMEM],
        out_specs=[VMEM] * 3,
        compiler_params=PARAMS,
        cost_estimate=COST,
        name="own_block",
    )(place, x, kv)


def more_block(shift, place, x, kv, state):
    return pl.pallas_call(
        functools.partial(more_kernel, shift),
        out_shape=STATE,
        in_specs=[SMEM] + [VMEM] * 5,
        out_specs=[VMEM] * 3,
        input_output_aliases={3: 0, 4: 1, 5: 2},
        compiler_params=PARAMS,
        cost_estimate=COST,
        name="more_block",
    )(place, x, kv, *state)


def last_block(shift, place, x, kv, state):
    return pl.pallas_call(
        functools.partial(last_kernel, shift),
        out_shape=[jax.ShapeDtypeStruct((ROWS, GROUP * HD), jnp.bfloat16)] + STATE,
        in_specs=[SMEM] + [VMEM] * 5,
        out_specs=[VMEM] * 4,
        input_output_aliases={3: 1, 4: 2, 5: 3},
        compiler_params=PARAMS,
        cost_estimate=COST,
        name="last_block",
    )(place, x, kv, *state)[0]


def local(queries, keys, values):
    rows = queries.shape[0]
    me = lax.axis_index("ctx")
    place = jnp.stack([me // (NY * NX), (me // NX) % NY]).astype(jnp.int32)
    by_head = jnp.concatenate(
        [
            queries.reshape(rows, KVH, GROUP * HD),
            keys.reshape(rows, KVH, HD),
            values.reshape(rows, KVH, HD),
        ],
        axis=2,
    ).transpose(1, 0, 2)
    x = lax.all_to_all(by_head, "ctx", 0, 0, axis_index_groups=X_GROUPS, tiled=True)
    x = x.reshape(ROWS, (GROUP + 2) * HD)
    kv = lax.all_gather(
        x[:, GROUP * HD :], "ctx", axis=0, tiled=True, axis_index_groups=Z_GROUPS
    )
    x = x[:, : GROUP * HD]
    up = down = kv
    arrived = []
    for step in range(1, NY // 2):
        up = lax.ppermute(up, "ctx", ring(1))
        down = lax.ppermute(down, "ctx", ring(-1))
        arrived += [(step, up), (-step, down)]
    up = lax.ppermute(up, "ctx", ring(1))
    state = own_block(place, x, kv)
    for shift, block in arrived:
        state = more_block(shift, place, x, block, state)
    out = last_block(NY // 2, place, x, up, state)
    out = lax.all_to_all(
        out.reshape(NX, rows, GROUP * HD),
        "ctx",
        0,
        0,
        axis_index_groups=X_GROUPS,
        tiled=True,
    )
    return out.transpose(1, 0, 2).reshape(rows, QH * HD)


def solution(mesh):
    spec = P(("dp", "ctx"), None)
    return jax.shard_map(
        local, mesh=mesh, in_specs=(spec,) * 3, out_specs=spec, check_vma=False
    )
```

```python
import functools
import math

import jax
import jax.numpy as jnp
from jax import lax
from jax.experimental import pallas as pl
from jax.experimental.pallas import tpu as pltpu
from jax.sharding import PartitionSpec as P

QH = 32
KVH = 4
HD = 128
GROUP = QH // KVH
NZ, NY, NX = 2, 8, 4
ROWS = 256
SCALE = math.log2(math.e) / math.sqrt(HD)
NEG = -1e30
QK = (((1,), (1,)), ((), ()))


def index(z, y, x):
    return z * (NY * NX) + y * NX + x


X_GROUPS = [[index(z, y, x) for x in range(NX)] for z in range(NZ) for y in range(NY)]
Z_GROUPS = [[index(z, y, x) for z in range(NZ)] for y in range(NY) for x in range(NX)]


def ring(step):
    return [
        (index(z, y, x), index(z, (y + step) % NY, x))
        for z in range(NZ)
        for y in range(NY)
        for x in range(NX)
    ]


def lane_sums(weights):
    total = weights[:, :HD]
    for at in range(HD, weights.shape[1], HD):
        total = total + weights[:, at : at + HD]
    return total


def scores_of(j, n, x_ref, kv_ref):
    return lax.dot_general(
        x_ref[:, j * HD : (j + 1) * HD],
        kv_ref[:n, :HD],
        QK,
        preferred_element_type=jnp.float32,
    )


def per_head(n, x_ref, kv_ref, finish):
    scores = scores_of(0, n, x_ref, kv_ref)
    for j in range(GROUP):
        ahead = scores_of(j + 1, n, x_ref, kv_ref) if j + 1 < GROUP else None
        finish(slice(j * HD, (j + 1) * HD), scores)
        scores = ahead


def own_kernel(place, x_ref, kv_ref, acc_ref, max_ref, sum_ref):
    shape = (ROWS, 2 * ROWS)
    row = lax.broadcasted_iota(jnp.int32, shape, 0)
    col = lax.broadcasted_iota(jnp.int32, shape, 1)
    seen = col <= row + place[0] * ROWS

    def finish(cols, scores):
        scores = jnp.where(seen, scores, NEG)
        peak = jnp.max(scores, axis=1, keepdims=True) * SCALE
        weights = jnp.exp2(scores * SCALE - peak)
        sum_ref[:, cols] = lane_sums(weights)
        acc_ref[:, cols] = jnp.dot(
            weights.astype(jnp.bfloat16),
            kv_ref[:, HD:],
            preferred_element_type=jnp.float32,
        )
        max_ref[:, cols] = jnp.broadcast_to(peak, (ROWS, HD))

    per_head(2 * ROWS, x_ref, kv_ref, finish)


def absorb(n, x_ref, kv_ref, acc_in, max_in, sum_in, acc_ref, max_ref, sum_ref):
    def finish(cols, scores):
        old = max_in[:, cols]
        peak = jnp.maximum(old, jnp.max(scores, axis=1, keepdims=True) * SCALE)
        keep = jnp.exp2(old - peak)
        weights = jnp.exp2(scores * SCALE - jnp.tile(peak, (1, n // HD)))
        sum_ref[:, cols] = sum_in[:, cols] * keep + lane_sums(weights)
        acc_ref[:, cols] = acc_in[:, cols] * keep + jnp.dot(
            weights.astype(jnp.bfloat16),
            kv_ref[:n, HD:],
            preferred_element_type=jnp.float32,
        )
        max_ref[:, cols] = peak

    per_head(n, x_ref, kv_ref, finish)


def absorb_if_needed(shift, place, x_ref, kv_ref, ins, outs):
    z, y = place[0], place[1]
    before = (lax.rem(y - shift + NY, NY) < y).astype(jnp.int32)

    @pl.when(z + before == 2)
    def _():
        absorb(2 * ROWS, x_ref, kv_ref, *ins, *outs)

    @pl.when(z + before == 1)
    def _():
        absorb(ROWS, x_ref, kv_ref, *ins, *outs)


def more_kernel(shift, place, x_ref, kv_ref, a_in, m_in, s_in, a_out, m_out, s_out):
    absorb_if_needed(
        shift, place, x_ref, kv_ref, (a_in, m_in, s_in), (a_out, m_out, s_out)
    )


def last_kernel(
    shift, place, x_ref, kv_ref, a_in, m_in, s_in, o_ref, a_out, m_out, s_out
):
    absorb_if_needed(
        shift, place, x_ref, kv_ref, (a_in, m_in, s_in), (a_out, m_out, s_out)
    )
    for j in range(GROUP):
        cols = slice(j * HD, (j + 1) * HD)
        total = jnp.sum(s_out[:, cols], axis=1, keepdims=True)
        o_ref[:, cols] = (a_out[:, cols] / total).astype(jnp.bfloat16)


VMEM = pl.BlockSpec(memory_space=pltpu.VMEM)
SMEM = pl.BlockSpec(memory_space=pltpu.SMEM)
STATE = [jax.ShapeDtypeStruct((ROWS, GROUP * HD), jnp.float32)] * 3
PARAMS = pltpu.CompilerParams(vmem_limit_bytes=24 << 20)
COST = pl.CostEstimate(
    flops=4 * ROWS * GROUP * 2 * ROWS * HD,
    bytes_accessed=8 << 20,
    transcendentals=ROWS * GROUP * 2 * ROWS,
)


def own_block(place, x, kv):
    return pl.pallas_call(
        own_kernel,
        out_shape=STATE,
        in_specs=[SMEM, VMEM, VMEM],
        out_specs=[VMEM] * 3,
        compiler_params=PARAMS,
        cost_estimate=COST,
        name="own_block",
    )(place, x, kv)


def more_block(shift, place, x, kv, state):
    return pl.pallas_call(
        functools.partial(more_kernel, shift),
        out_shape=STATE,
        in_specs=[SMEM] + [VMEM] * 5,
        out_specs=[VMEM] * 3,
        input_output_aliases={3: 0, 4: 1, 5: 2},
        compiler_params=PARAMS,
        cost_estimate=COST,
        name="more_block",
    )(place, x, kv, *state)


def last_block(shift, place, x, kv, state):
    return pl.pallas_call(
        functools.partial(last_kernel, shift),
        out_shape=[jax.ShapeDtypeStruct((ROWS, GROUP * HD), jnp.bfloat16)] + STATE,
        in_specs=[SMEM] + [VMEM] * 5,
        out_specs=[VMEM] * 4,
        input_output_aliases={3: 1, 4: 2, 5: 3},
        compiler_params=PARAMS,
        cost_estimate=COST,
        name="last_block",
    )(place, x, kv, *state)[0]


def local(queries, keys, values):
    rows = queries.shape[0]
    me = lax.axis_index("ctx")
    place = jnp.stack([me // (NY * NX), (me // NX) % NY]).astype(jnp.int32)
    by_head = jnp.concatenate(
        [
            queries.reshape(rows, KVH, GROUP * HD),
            keys.reshape(rows, KVH, HD),
            values.reshape(rows, KVH, HD),
        ],
        axis=2,
    ).transpose(1, 0, 2)
    x = lax.all_to_all(by_head, "ctx", 0, 0, axis_index_groups=X_GROUPS, tiled=True)
    x = x.reshape(ROWS, (GROUP + 2) * HD)
    kv = lax.all_gather(
        x[:, GROUP * HD :], "ctx", axis=0, tiled=True, axis_index_groups=Z_GROUPS
    )
    x = x[:, : GROUP * HD]
    up = lax.ppermute(kv, "ctx", ring(1))
    down = lax.ppermute(kv, "ctx", ring(-1))
    state = own_block(place, x, kv)
    for step in range(1, NY // 2):
        up, state = lax.optimization_barrier((up, state))
        next_up = lax.ppermute(up, "ctx", ring(1))
        state = more_block(step, place, x, up, state)
        if step + 1 < NY // 2:
            down, state = lax.optimization_barrier((down, state))
            next_down = lax.ppermute(down, "ctx", ring(-1))
        state = more_block(-step, place, x, down, state)
        up, down = next_up, next_down
    out = last_block(NY // 2, place, x, up, state)
    out = lax.all_to_all(
        out.reshape(NX, rows, GROUP * HD),
        "ctx",
        0,
        0,
        axis_index_groups=X_GROUPS,
        tiled=True,
    )
    return out.transpose(1, 0, 2).reshape(rows, QH * HD)


def solution(mesh):
    spec = P(("dp", "ctx"), None)
    return jax.shard_map(
        local, mesh=mesh, in_specs=(spec,) * 3, out_specs=spec, check_vma=False
    )
```

```python
import functools
import math

import jax
import jax.numpy as jnp
from jax import lax
from jax.experimental import pallas as pl
from jax.experimental.pallas import tpu as pltpu
from jax.sharding import PartitionSpec as P

QH = 32
KVH = 4
HD = 128
GROUP = QH // KVH
NZ, NY, NX = 2, 8, 4
ROWS = 256
SCALE = math.log2(math.e) / math.sqrt(HD)
NEG = -1e30
HIDE = 1e30
QK = (((1,), (1,)), ((), ()))


def index(z, y, x):
    return z * (NY * NX) + y * NX + x


X_GROUPS = [[index(z, y, x) for x in range(NX)] for z in range(NZ) for y in range(NY)]
Z_UP = [(index(0, y, x), index(1, y, x)) for y in range(NY) for x in range(NX)]


def ring(step):
    return [
        (index(z, y, x), index(z, (y + step) % NY, x))
        for z in range(NZ)
        for y in range(NY)
        for x in range(NX)
    ]


def lane_sums(weights):
    total = weights[:, :HD]
    for at in range(HD, weights.shape[1], HD):
        total = total + weights[:, at : at + HD]
    return total


def joined(blocks, column):
    return jnp.concatenate(
        [
            block[:, at + column : at + column + HD]
            for block in blocks
            for at in (0, 2 * HD)
        ],
        axis=0,
    )


def per_head(x_ref, blocks, finish):
    def scores_of(j):
        return lax.dot_general(
            x_ref[:, j * HD : (j + 1) * HD],
            joined(blocks, 0),
            QK,
            preferred_element_type=jnp.float32,
        )

    scores = scores_of(0)
    for j in range(GROUP):
        ahead = scores_of(j + 1) if j + 1 < GROUP else None
        finish(slice(j * HD, (j + 1) * HD), scores)
        scores = ahead


def mixed(weights, blocks):
    return jnp.dot(
        weights.astype(jnp.bfloat16),
        joined(blocks, HD),
        preferred_element_type=jnp.float32,
    )


def own_kernel(place, x_ref, kv_ref, acc_ref, max_ref, sum_ref):
    shape = (ROWS, 2 * ROWS)
    row = lax.broadcasted_iota(jnp.int32, shape, 0)
    col = lax.broadcasted_iota(jnp.int32, shape, 1)
    seen = col <= row + place[0] * ROWS

    def finish(cols, scores):
        scores = jnp.where(seen, scores, NEG)
        peak = jnp.max(scores, axis=1, keepdims=True) * SCALE
        weights = jnp.exp2(scores * SCALE - peak)
        sum_ref[:, cols] = lane_sums(weights)
        acc_ref[:, cols] = mixed(weights, [kv_ref])
        max_ref[:, cols] = jnp.broadcast_to(peak, (ROWS, HD))

    per_head(x_ref, [kv_ref], finish)


def absorb(shifts, place, x_ref, blocks, ins, outs, done=None):
    z, y = place[0], place[1]
    hidden = []
    for shift in shifts:
        before = (lax.rem(y - shift + NY, NY) < y).astype(jnp.int32)
        hidden.append(jnp.where(z + before >= 1, 0.0, HIDE))
        hidden.append(jnp.where(z + before == 2, 0.0, HIDE))
    acc_in, max_in, sum_in = ins
    acc_ref, max_ref, sum_ref = outs

    def finish(cols, scores):
        old = max_in[:, cols]
        top = None
        for c, gap in enumerate(hidden):
            left = scores[:, c * ROWS : c * ROWS + HD]
            right = scores[:, c * ROWS + HD : (c + 1) * ROWS]
            here = jnp.maximum(left, right) * SCALE - gap
            top = here if top is None else jnp.maximum(top, here)
        peak = jnp.maximum(old, jnp.max(top, axis=1, keepdims=True))
        keep = jnp.exp2(old - peak)
        base = jnp.concatenate([peak + gap for gap in hidden for _ in (0, 1)], axis=1)
        weights = jnp.exp2(scores * SCALE - base)
        total = sum_in[:, cols] * keep + lane_sums(weights)
        acc = acc_in[:, cols] * keep + mixed(weights, blocks)
        if done is None:
            sum_ref[:, cols] = total
            acc_ref[:, cols] = acc
            max_ref[:, cols] = peak
        else:
            total = jnp.sum(total, axis=1, keepdims=True)
            done[:, cols] = (acc / total).astype(jnp.bfloat16)

    per_head(x_ref, blocks, finish)


def pair_kernel(step, place, x_ref, up_ref, down_ref, a, m, s, a_out, m_out, s_out):
    absorb(
        (step, -step), place, x_ref, [up_ref, down_ref], (a, m, s), (a_out, m_out, s_out)
    )


def last_kernel(step, place, x_ref, up_ref, a, m, s, o_ref):
    absorb((step,), place, x_ref, [up_ref], (a, m, s), (None,) * 3, o_ref)


VMEM = pl.BlockSpec(memory_space=pltpu.VMEM)
SMEM = pl.BlockSpec(memory_space=pltpu.SMEM)
STATE = [jax.ShapeDtypeStruct((ROWS, GROUP * HD), jnp.float32)] * 3
PARAMS = pltpu.CompilerParams(vmem_limit_bytes=32 << 20)


def cost(blocks):
    pairs = ROWS * GROUP * 2 * ROWS * blocks
    return pl.CostEstimate(
        flops=4 * pairs * HD, bytes_accessed=8 << 20, transcendentals=pairs
    )


def own_block(place, x, kv):
    return pl.pallas_call(
        own_kernel,
        out_shape=STATE,
        in_specs=[SMEM, VMEM, VMEM],
        out_specs=[VMEM] * 3,
        compiler_params=PARAMS,
        cost_estimate=cost(1),
        name="own_block",
    )(place, x, kv)


def pair_block(step, place, x, up, down, state):
    return pl.pallas_call(
        functools.partial(pair_kernel, step),
        out_shape=STATE,
        in_specs=[SMEM] + [VMEM] * 6,
        out_specs=[VMEM] * 3,
        input_output_aliases={4: 0, 5: 1, 6: 2},
        compiler_params=PARAMS,
        cost_estimate=cost(2),
        name="pair_block",
    )(place, x, up, down, *state)


def last_block(step, place, x, up, state):
    return pl.pallas_call(
        functools.partial(last_kernel, step),
        out_shape=jax.ShapeDtypeStruct((ROWS, GROUP * HD), jnp.bfloat16),
        in_specs=[SMEM] + [VMEM] * 5,
        out_specs=VMEM,
        compiler_params=PARAMS,
        cost_estimate=cost(1),
        name="last_block",
    )(place, x, up, *state)


def local(queries, keys, values):
    rows = queries.shape[0]
    me = lax.axis_index("ctx")
    z, y = me // (NY * NX), (me // NX) % NY
    place = jnp.stack([z, y]).astype(jnp.int32)
    own = jnp.concatenate(
        [keys.reshape(rows, KVH, HD), values.reshape(rows, KVH, HD)], axis=2
    )
    first = lax.ppermute(own, "ctx", Z_UP)
    first = jnp.where(z == 0, own, first)
    by_head = jnp.concatenate(
        [queries.reshape(rows, KVH, GROUP * HD), first, own], axis=2
    ).transpose(1, 0, 2)
    x = lax.all_to_all(by_head, "ctx", 0, 0, axis_index_groups=X_GROUPS, tiled=True)
    x = x.reshape(ROWS, (GROUP + 4) * HD)
    kv = x[:, GROUP * HD :]
    x = x[:, : GROUP * HD]
    up = lax.ppermute(kv, "ctx", ring(1))
    down = lax.ppermute(kv, "ctx", ring(-1))
    state = own_block(place, x, kv)
    for step in range(1, NY // 2):
        up, state = lax.optimization_barrier((up, state))
        next_up = lax.ppermute(up, "ctx", ring(1))
        if step + 1 < NY // 2:
            next_down = lax.ppermute(down, "ctx", ring(-1))
        state = pair_block(step, place, x, up, down, state)
        up, down = next_up, next_down
    out = last_block(NY // 2, place, x, up, state)
    out = lax.all_to_all(
        out.reshape(NX, rows, GROUP * HD),
        "ctx",
        0,
        0,
        axis_index_groups=X_GROUPS,
        tiled=True,
    )
    return out.transpose(1, 0, 2).reshape(rows, QH * HD)


def solution(mesh):
    spec = P(("dp", "ctx"), None)
    return jax.shard_map(
        local, mesh=mesh, in_specs=(spec,) * 3, out_specs=spec, check_vma=False
    )
```

```python
import functools
import math

import jax
import jax.numpy as jnp
from jax import lax
from jax.experimental import pallas as pl
from jax.experimental.pallas import tpu as pltpu
from jax.sharding import PartitionSpec as P

QH = 32
KVH = 4
HD = 128
GROUP = QH // KVH
NZ, NY, NX = 2, 8, 4
ROWS = 256
SCALE = math.log2(math.e) / math.sqrt(HD)
NEG = -1e30
QK = (((1,), (1,)), ((), ()))


def index(z, y, x):
    return z * (NY * NX) + y * NX + x


X_GROUPS = [[index(z, y, x) for x in range(NX)] for z in range(NZ) for y in range(NY)]
Z_GROUPS = [[index(z, y, x) for z in range(NZ)] for y in range(NY) for x in range(NX)]


def ring(step):
    return [
        (index(z, y, x), index(z, (y + step) % NY, x))
        for z in range(NZ)
        for y in range(NY)
        for x in range(NX)
    ]


def per_head(x_ref, keys_of, finish):
    def scores_of(j):
        return lax.dot_general(
            x_ref[:, j * HD : (j + 1) * HD],
            keys_of(),
            QK,
            preferred_element_type=jnp.float32,
        )

    scores = scores_of(0)
    for j in range(GROUP):
        ahead = scores_of(j + 1) if j + 1 < GROUP else None
        finish(slice(j * HD, (j + 1) * HD), scores)
        scores = ahead


def weigh(weights, value_scr):
    both = jnp.dot(
        weights.astype(jnp.bfloat16),
        value_scr[...],
        preferred_element_type=jnp.float32,
    )
    return both[:, :HD], both[:, HD:]


def own_kernel(place, x_ref, kv_ref, acc_ref, max_ref, sum_ref, key_scr, value_scr):
    value_scr[:, HD:] = jnp.ones((2 * ROWS, HD), jnp.bfloat16)
    key_scr[...] = kv_ref[:, :HD]
    value_scr[:, :HD] = kv_ref[:, HD:]
    shape = (ROWS, 2 * ROWS)
    row = lax.broadcasted_iota(jnp.int32, shape, 0)
    col = lax.broadcasted_iota(jnp.int32, shape, 1)
    seen = col <= row + place[0] * ROWS

    def finish(cols, scores):
        scores = jnp.where(seen, scores, NEG)
        peak = jnp.max(scores, axis=1, keepdims=True) * SCALE
        weights = jnp.exp2(scores * SCALE - peak)
        acc_ref[:, cols], sum_ref[:, cols] = weigh(weights, value_scr)
        max_ref[:, cols] = jnp.broadcast_to(peak, (ROWS, HD))

    per_head(x_ref, lambda: key_scr[...], finish)


def more_kernel(shifts, last, *refs):
    n = len(shifts)
    place, x_ref, blocks = refs[0], refs[1], refs[2 : 2 + n]
    acc_in, max_in, sum_in = refs[2 + n : 5 + n]
    outs, (key_scr, value_scr, safe_scr) = refs[5 + n : -3], refs[-3:]
    z, y = place[0], place[1]
    allowed = []
    for shift in shifts:
        before = (lax.rem(y - shift + NY, NY) < y).astype(jnp.int32)
        allowed += [z + before >= 1, z + before == 2]
    any_allowed = functools.reduce(jnp.logical_or, allowed)

    def put(c, key, value, one):
        key_scr[c * ROWS : (c + 1) * ROWS, :] = key
        value_scr[c * ROWS : (c + 1) * ROWS, :HD] = value
        value_scr[c * ROWS : (c + 1) * ROWS, HD:] = one

    @pl.when(any_allowed)
    def _():
        for c in range(2 * n - 2, -1, -2):

            @pl.when(allowed[c])
            def _(c=c):
                safe_scr[...] = blocks[c // 2][:ROWS, :HD]

        one = jnp.ones((ROWS, HD), jnp.bfloat16)
        for c in range(2 * n):
            block, at = blocks[c // 2], c % 2 * ROWS

            @pl.when(allowed[c])
            def _(c=c, block=block, at=at):
                put(c, block[at : at + ROWS, :HD], block[at : at + ROWS, HD:], one)

            @pl.when(jnp.logical_not(allowed[c]))
            def _(c=c):
                put(c, safe_scr[...], jnp.zeros_like(one), jnp.zeros_like(one))

        def finish(cols, scores):
            old = max_in[:, cols]
            peak = jnp.maximum(old, jnp.max(scores, axis=1, keepdims=True) * SCALE)
            keep = jnp.exp2(old - peak)
            weights = jnp.exp2(scores * SCALE - jnp.tile(peak, (1, 4 * n)))
            acc, total = weigh(weights, value_scr)
            acc = acc_in[:, cols] * keep + acc
            total = sum_in[:, cols] * keep + total
            if last:
                outs[0][:, cols] = (acc / total).astype(jnp.bfloat16)
            else:
                outs[0][:, cols], outs[1][:, cols], outs[2][:, cols] = acc, peak, total

        per_head(x_ref, lambda: key_scr[...], finish)

    if last:

        @pl.when(jnp.logical_not(any_allowed))
        def _():
            outs[0][...] = (acc_in[...] / sum_in[...]).astype(jnp.bfloat16)


VMEM = pl.BlockSpec(memory_space=pltpu.VMEM)
SMEM = pl.BlockSpec(memory_space=pltpu.SMEM)
STATE = [jax.ShapeDtypeStruct((ROWS, GROUP * HD), jnp.float32)] * 3
PARAMS = pltpu.CompilerParams(vmem_limit_bytes=32 << 20)


def cost(blocks):
    pairs = ROWS * GROUP * 2 * ROWS * blocks
    return pl.CostEstimate(
        flops=4 * pairs * HD, bytes_accessed=8 << 20, transcendentals=pairs
    )


def scratch(blocks):
    return [
        pltpu.VMEM((2 * ROWS * blocks, HD), jnp.bfloat16),
        pltpu.VMEM((2 * ROWS * blocks, 2 * HD), jnp.bfloat16),
    ]


def own_block(place, x, kv):
    return pl.pallas_call(
        own_kernel,
        out_shape=STATE,
        in_specs=[SMEM, VMEM, VMEM],
        out_specs=[VMEM] * 3,
        scratch_shapes=scratch(1),
        compiler_params=PARAMS,
        cost_estimate=cost(1),
        name="own_block",
    )(place, x, kv)


def more_blocks(arrived, place, x, state):
    shifts = tuple(shift for shift, _ in arrived)
    n = len(arrived)
    return pl.pallas_call(
        functools.partial(more_kernel, shifts, False),
        out_shape=STATE,
        in_specs=[SMEM] + [VMEM] * (n + 4),
        out_specs=[VMEM] * 3,
        scratch_shapes=scratch(n) + [pltpu.VMEM((ROWS, HD), jnp.bfloat16)],
        input_output_aliases={n + 2: 0, n + 3: 1, n + 4: 2},
        compiler_params=PARAMS,
        cost_estimate=cost(n),
        name="more_blocks",
    )(place, x, *[block for _, block in arrived], *state)


def last_blocks(arrived, place, x, state):
    shifts = tuple(shift for shift, _ in arrived)
    n = len(arrived)
    return pl.pallas_call(
        functools.partial(more_kernel, shifts, True),
        out_shape=[jax.ShapeDtypeStruct((ROWS, GROUP * HD), jnp.bfloat16)],
        in_specs=[SMEM] + [VMEM] * (n + 4),
        out_specs=[VMEM],
        scratch_shapes=scratch(n) + [pltpu.VMEM((ROWS, HD), jnp.bfloat16)],
        compiler_params=PARAMS,
        cost_estimate=cost(n),
        name="last_blocks",
    )(place, x, *[block for _, block in arrived], *state)[0]


def local(queries, keys, values):
    rows = queries.shape[0]
    me = lax.axis_index("ctx")
    z, y = me // (NY * NX), (me // NX) % NY
    place = jnp.stack([z, y]).astype(jnp.int32)
    by_head = jnp.concatenate(
        [
            queries.reshape(rows, KVH, GROUP * HD),
            keys.reshape(rows, KVH, HD),
            values.reshape(rows, KVH, HD),
        ],
        axis=2,
    ).transpose(1, 0, 2)
    x = lax.all_to_all(by_head, "ctx", 0, 0, axis_index_groups=X_GROUPS, tiled=True)
    x = x.reshape(ROWS, (GROUP + 2) * HD)
    kv = lax.all_gather(
        x[:, GROUP * HD :], "ctx", axis=0, tiled=True, axis_index_groups=Z_GROUPS
    )
    x = x[:, : GROUP * HD]
    got = {}
    got[1] = lax.ppermute(kv, "ctx", ring(1))
    got[-1] = lax.ppermute(kv, "ctx", ring(-1))
    state = own_block(place, x, kv)
    for step, shifts in ((1, (1,)), (2, (-1, 2)), (3, (-2, 3, -3))):
        got[step], state = lax.optimization_barrier((got[step], state))
        got[step + 1] = lax.ppermute(got[step], "ctx", ring(1))
        if step < NY // 2 - 1:
            got[-step - 1] = lax.ppermute(got[-step], "ctx", ring(-1))
        state = more_blocks([(at, got[at]) for at in shifts], place, x, state)
    out = last_blocks([(NY // 2, got[NY // 2])], place, x, state)
    out = lax.all_to_all(
        out.reshape(NX, rows, GROUP * HD),
        "ctx",
        0,
        0,
        axis_index_groups=X_GROUPS,
        tiled=True,
    )
    return out.transpose(1, 0, 2).reshape(rows, QH * HD)


def solution(mesh):
    spec = P(("dp", "ctx"), None)
    return jax.shard_map(
        local, mesh=mesh, in_specs=(spec,) * 3, out_specs=spec, check_vma=False
    )
```

```python
import functools
import math

import jax
import jax.numpy as jnp
from jax import lax
from jax.experimental import pallas as pl
from jax.experimental.pallas import tpu as pltpu
from jax.sharding import PartitionSpec as P

QH = 32
KVH = 4
HD = 128
GROUP = QH // KVH
NZ, NY, NX = 2, 8, 4
ROWS = 256
SCALE = math.log2(math.e) / math.sqrt(HD)
NEG = -1e30
QK = (((1,), (1,)), ((), ()))


def index(z, y, x):
    return z * (NY * NX) + y * NX + x


X_GROUPS = [[index(z, y, x) for x in range(NX)] for z in range(NZ) for y in range(NY)]
Z_SWAP = [
    (index(z, y, x), index(1 - z, y, x))
    for z in range(NZ)
    for y in range(NY)
    for x in range(NX)
]


def exchange(pieces):
    return lax.all_to_all(
        pieces, "ctx", 0, 0, axis_index_groups=X_GROUPS, tiled=True
    )


def ring(step):
    return [
        (index(z, y, x), index(z, (y + step) % NY, x))
        for z in range(NZ)
        for y in range(NY)
        for x in range(NX)
    ]


def per_head(x_ref, keys_of, finish):
    def scores_of(j):
        return lax.dot_general(
            x_ref[:, j * HD : (j + 1) * HD],
            keys_of(),
            QK,
            preferred_element_type=jnp.float32,
        )

    scores = scores_of(0)
    for j in range(GROUP):
        ahead = scores_of(j + 1) if j + 1 < GROUP else None
        finish(slice(j * HD, (j + 1) * HD), scores)
        scores = ahead


def weigh(weights, value_scr):
    both = jnp.dot(
        weights.astype(jnp.bfloat16),
        value_scr[...],
        preferred_element_type=jnp.float32,
    )
    return both[:, :HD], both[:, HD:]


def own_kernel(place, x_ref, kv_ref, acc_ref, max_ref, sum_ref, key_scr, value_scr):
    value_scr[:, HD:] = jnp.ones((2 * ROWS, HD), jnp.bfloat16)
    key_scr[...] = kv_ref[:, :HD]
    value_scr[:, :HD] = kv_ref[:, HD:]
    shape = (ROWS, 2 * ROWS)
    row = lax.broadcasted_iota(jnp.int32, shape, 0)
    col = lax.broadcasted_iota(jnp.int32, shape, 1)
    seen = col <= row + place[0] * ROWS

    def finish(cols, scores):
        scores = jnp.where(seen, scores, NEG)
        peak = jnp.max(scores, axis=1, keepdims=True) * SCALE
        weights = jnp.exp2(scores * SCALE - peak)
        acc_ref[:, cols], sum_ref[:, cols] = weigh(weights, value_scr)
        max_ref[:, cols] = jnp.broadcast_to(peak, (ROWS, HD))

    per_head(x_ref, lambda: key_scr[...], finish)


def more_kernel(shifts, last, *refs):
    n = len(shifts)
    place, x_ref, blocks = refs[0], refs[1], refs[2 : 2 + n]
    acc_in, max_in, sum_in = refs[2 + n : 5 + n]
    outs, (key_scr, value_scr) = refs[5 + n : -2], refs[-2:]
    z, y = place[0], place[1]
    allowed = []
    for shift in shifts:
        before = (lax.rem(y - shift + NY, NY) < y).astype(jnp.int32)
        allowed += [z + before >= 1, z + before == 2]
    any_allowed = functools.reduce(jnp.logical_or, allowed)

    @pl.when(any_allowed)
    def _():
        safe = blocks[n - 1][:ROWS, :HD]
        for b in range(n - 2, -1, -1):
            safe = jnp.where(allowed[2 * b], blocks[b][:ROWS, :HD], safe)
        for c, seen in enumerate(allowed):
            block, at = blocks[c // 2], c % 2 * ROWS
            rows = slice(c * ROWS, (c + 1) * ROWS)
            value = block[at : at + ROWS, HD:]
            key_scr[rows, :] = jnp.where(seen, block[at : at + ROWS, :HD], safe)
            value_scr[rows, :HD] = jnp.where(seen, value, jnp.zeros_like(value))
            value_scr[rows, HD:] = jnp.where(
                seen, jnp.ones_like(value), jnp.zeros_like(value)
            )

        def finish(cols, scores):
            old = max_in[:, cols]
            peak = jnp.maximum(old, jnp.max(scores, axis=1, keepdims=True) * SCALE)
            keep = jnp.exp2(old - peak)
            weights = jnp.exp2(scores * SCALE - jnp.tile(peak, (1, 4 * n)))
            acc, total = weigh(weights, value_scr)
            acc = acc_in[:, cols] * keep + acc
            total = sum_in[:, cols] * keep + total
            if last:
                outs[0][:, cols] = (acc / total).astype(jnp.bfloat16)
            else:
                outs[0][:, cols], outs[1][:, cols], outs[2][:, cols] = acc, peak, total

        per_head(x_ref, lambda: key_scr[...], finish)

    if last:

        @pl.when(jnp.logical_not(any_allowed))
        def _():
            outs[0][...] = (acc_in[...] / sum_in[...]).astype(jnp.bfloat16)


VMEM = pl.BlockSpec(memory_space=pltpu.VMEM)
SMEM = pl.BlockSpec(memory_space=pltpu.SMEM)
STATE = [jax.ShapeDtypeStruct((ROWS, GROUP * HD), jnp.float32)] * 3
PARAMS = pltpu.CompilerParams(vmem_limit_bytes=32 << 20)


def cost(blocks):
    pairs = ROWS * GROUP * 2 * ROWS * blocks
    return pl.CostEstimate(
        flops=4 * pairs * HD, bytes_accessed=8 << 20, transcendentals=pairs
    )


def scratch(blocks):
    return [
        pltpu.VMEM((2 * ROWS * blocks, HD), jnp.bfloat16),
        pltpu.VMEM((2 * ROWS * blocks, 2 * HD), jnp.bfloat16),
    ]


def own_block(place, x, kv):
    return pl.pallas_call(
        own_kernel,
        out_shape=STATE,
        in_specs=[SMEM, VMEM, VMEM],
        out_specs=[VMEM] * 3,
        scratch_shapes=scratch(1),
        compiler_params=PARAMS,
        cost_estimate=cost(1),
        name="own_block",
    )(place, x, kv)


def more_blocks(arrived, place, x, state):
    shifts = tuple(shift for shift, _ in arrived)
    n = len(arrived)
    return pl.pallas_call(
        functools.partial(more_kernel, shifts, False),
        out_shape=STATE,
        in_specs=[SMEM] + [VMEM] * (n + 4),
        out_specs=[VMEM] * 3,
        scratch_shapes=scratch(n),
        input_output_aliases={n + 2: 0, n + 3: 1, n + 4: 2},
        compiler_params=PARAMS,
        cost_estimate=cost(n),
        name="more_blocks",
    )(place, x, *[block for _, block in arrived], *state)


def last_blocks(arrived, place, x, state):
    shifts = tuple(shift for shift, _ in arrived)
    n = len(arrived)
    return pl.pallas_call(
        functools.partial(more_kernel, shifts, True),
        out_shape=[jax.ShapeDtypeStruct((ROWS, GROUP * HD), jnp.bfloat16)],
        in_specs=[SMEM] + [VMEM] * (n + 4),
        out_specs=[VMEM],
        scratch_shapes=scratch(n),
        compiler_params=PARAMS,
        cost_estimate=cost(n),
        name="last_blocks",
    )(place, x, *[block for _, block in arrived], *state)[0]


def local(queries, keys, values):
    rows = queries.shape[0]
    me = lax.axis_index("ctx")
    z, y = me // (NY * NX), (me // NX) % NY
    place = jnp.stack([z, y]).astype(jnp.int32)
    by_head = jnp.concatenate(
        [keys.reshape(rows, KVH, HD), values.reshape(rows, KVH, HD)], axis=2
    ).transpose(1, 0, 2)
    own = exchange(by_head).reshape(ROWS, 2 * HD)
    other = lax.ppermute(own, "ctx", Z_SWAP)
    x = exchange(queries.reshape(rows, KVH, GROUP * HD).transpose(1, 0, 2))
    x = x.reshape(ROWS, GROUP * HD)
    kv = jnp.concatenate(
        [jnp.where(z == 0, own, other), jnp.where(z == 0, other, own)], axis=0
    )
    got = {}
    got[1] = lax.ppermute(kv, "ctx", ring(1))
    got[-1] = lax.ppermute(kv, "ctx", ring(-1))
    state = own_block(place, x, kv)
    for step, shifts in ((1, (1,)), (2, (-1, 2)), (3, (-2, 3, -3))):
        got[step], state = lax.optimization_barrier((got[step], state))
        got[step + 1] = lax.ppermute(got[step], "ctx", ring(1))
        if step < NY // 2 - 1:
            got[-step - 1] = lax.ppermute(got[-step], "ctx", ring(-1))
        state = more_blocks([(at, got[at]) for at in shifts], place, x, state)
    out = last_blocks([(NY // 2, got[NY // 2])], place, x, state)
    out = exchange(out.reshape(NX, rows, GROUP * HD))
    return out.transpose(1, 0, 2).reshape(rows, QH * HD)


def solution(mesh):
    spec = P(("dp", "ctx"), None)
    return jax.shard_map(
        local, mesh=mesh, in_specs=(spec,) * 3, out_specs=spec, check_vma=False
    )
```

```python
import functools
import math

import jax
import jax.numpy as jnp
from jax import lax
from jax.experimental import pallas as pl
from jax.experimental.pallas import tpu as pltpu
from jax.sharding import PartitionSpec as P

QH = 32
KVH = 4
HD = 128
GROUP = QH // KVH
NZ, NY, NX = 2, 8, 4
ROWS = 256
SCALE = math.log2(math.e) / math.sqrt(HD)
NEG = -1e30
QK = (((1,), (1,)), ((), ()))


def index(z, y, x):
    return z * (NY * NX) + y * NX + x


X_GROUPS = [[index(z, y, x) for x in range(NX)] for z in range(NZ) for y in range(NY)]
Z_SWAP = [
    (index(z, y, x), index(1 - z, y, x))
    for z in range(NZ)
    for y in range(NY)
    for x in range(NX)
]


def place_of():
    me = lax.axis_index("ctx")
    return me // (NY * NX), lax.rem(me // NX, NY)


def exchange(pieces):
    return lax.all_to_all(
        pieces, "ctx", 0, 0, axis_index_groups=X_GROUPS, tiled=True
    )


def ring(step):
    return [
        (index(z, y, x), index(z, (y + step) % NY, x))
        for z in range(NZ)
        for y in range(NY)
        for x in range(NX)
    ]


def per_head(x_ref, keys_of, finish):
    def scores_of(j):
        return lax.dot_general(
            x_ref[:, j * HD : (j + 1) * HD],
            keys_of(),
            QK,
            preferred_element_type=jnp.float32,
        )

    scores = scores_of(0)
    for j in range(GROUP):
        ahead = scores_of(j + 1) if j + 1 < GROUP else None
        finish(slice(j * HD, (j + 1) * HD), scores)
        scores = ahead


def weigh(weights, value_scr):
    both = jnp.dot(
        weights.astype(jnp.bfloat16),
        value_scr[...],
        preferred_element_type=jnp.float32,
    )
    return both[:, :HD], both[:, HD:]


def own_kernel(x_ref, kv_ref, acc_ref, max_ref, sum_ref, key_scr, value_scr):
    value_scr[:, HD:] = jnp.ones((2 * ROWS, HD), jnp.bfloat16)
    key_scr[...] = kv_ref[:, :HD]
    value_scr[:, :HD] = kv_ref[:, HD:]
    shape = (ROWS, 2 * ROWS)
    row = lax.broadcasted_iota(jnp.int32, shape, 0)
    col = lax.broadcasted_iota(jnp.int32, shape, 1)
    seen = col <= row + place_of()[0] * ROWS

    def finish(cols, scores):
        scores = jnp.where(seen, scores, NEG)
        peak = jnp.max(scores, axis=1, keepdims=True) * SCALE
        weights = jnp.exp2(scores * SCALE - peak)
        acc_ref[:, cols], sum_ref[:, cols] = weigh(weights, value_scr)
        max_ref[:, cols] = jnp.broadcast_to(peak, (ROWS, HD))

    per_head(x_ref, lambda: key_scr[...], finish)


def more_kernel(shifts, last, *refs):
    n = len(shifts)
    x_ref, blocks = refs[0], refs[1 : 1 + n]
    acc_in, max_in, sum_in = refs[1 + n : 4 + n]
    outs, (key_scr, value_scr) = refs[4 + n : -2], refs[-2:]
    z, y = place_of()
    allowed = []
    for shift in shifts:
        before = (lax.rem(y - shift + NY, NY) < y).astype(jnp.int32)
        allowed += [z + before >= 1, z + before == 2]
    any_allowed = functools.reduce(jnp.logical_or, allowed)

    @pl.when(any_allowed)
    def _():
        safe = blocks[n - 1][:ROWS, :HD]
        for b in range(n - 2, -1, -1):
            safe = jnp.where(allowed[2 * b], blocks[b][:ROWS, :HD], safe)
        for c, seen in enumerate(allowed):
            block, at = blocks[c // 2], c % 2 * ROWS
            rows = slice(c * ROWS, (c + 1) * ROWS)
            value = block[at : at + ROWS, HD:]
            key_scr[rows, :] = jnp.where(seen, block[at : at + ROWS, :HD], safe)
            value_scr[rows, :HD] = jnp.where(seen, value, jnp.zeros_like(value))
            value_scr[rows, HD:] = jnp.where(
                seen, jnp.ones_like(value), jnp.zeros_like(value)
            )

        def finish(cols, scores):
            old = max_in[:, cols]
            peak = jnp.maximum(old, jnp.max(scores, axis=1, keepdims=True) * SCALE)
            keep = jnp.exp2(old - peak)
            weights = jnp.exp2(scores * SCALE - jnp.tile(peak, (1, 4 * n)))
            acc, total = weigh(weights, value_scr)
            acc = acc_in[:, cols] * keep + acc
            total = sum_in[:, cols] * keep + total
            if last:
                outs[0][:, cols] = (acc / total).astype(jnp.bfloat16)
            else:
                outs[0][:, cols], outs[1][:, cols], outs[2][:, cols] = acc, peak, total

        per_head(x_ref, lambda: key_scr[...], finish)

    if last:

        @pl.when(jnp.logical_not(any_allowed))
        def _():
            outs[0][...] = (acc_in[...] / sum_in[...]).astype(jnp.bfloat16)


VMEM = pl.BlockSpec(memory_space=pltpu.VMEM)
STATE = [jax.ShapeDtypeStruct((ROWS, GROUP * HD), jnp.float32)] * 3
PARAMS = pltpu.CompilerParams(vmem_limit_bytes=32 << 20)


def cost(blocks):
    pairs = ROWS * GROUP * 2 * ROWS * blocks
    return pl.CostEstimate(
        flops=4 * pairs * HD, bytes_accessed=8 << 20, transcendentals=pairs
    )


def scratch(blocks):
    return [
        pltpu.VMEM((2 * ROWS * blocks, HD), jnp.bfloat16),
        pltpu.VMEM((2 * ROWS * blocks, 2 * HD), jnp.bfloat16),
    ]


def own_block(x, kv):
    return pl.pallas_call(
        own_kernel,
        out_shape=STATE,
        in_specs=[VMEM, VMEM],
        out_specs=[VMEM] * 3,
        scratch_shapes=scratch(1),
        compiler_params=PARAMS,
        cost_estimate=cost(1),
        name="own_block",
    )(x, kv)


def more_blocks(arrived, x, state):
    shifts = tuple(shift for shift, _ in arrived)
    n = len(arrived)
    return pl.pallas_call(
        functools.partial(more_kernel, shifts, False),
        out_shape=STATE,
        in_specs=[VMEM] * (n + 4),
        out_specs=[VMEM] * 3,
        scratch_shapes=scratch(n),
        input_output_aliases={n + 1: 0, n + 2: 1, n + 3: 2},
        compiler_params=PARAMS,
        cost_estimate=cost(n),
        name="more_blocks",
    )(x, *[block for _, block in arrived], *state)


def last_blocks(arrived, x, state):
    shifts = tuple(shift for shift, _ in arrived)
    n = len(arrived)
    return pl.pallas_call(
        functools.partial(more_kernel, shifts, True),
        out_shape=[jax.ShapeDtypeStruct((ROWS, GROUP * HD), jnp.bfloat16)],
        in_specs=[VMEM] * (n + 4),
        out_specs=[VMEM],
        scratch_shapes=scratch(n),
        compiler_params=PARAMS,
        cost_estimate=cost(n),
        name="last_blocks",
    )(x, *[block for _, block in arrived], *state)[0]


def local(queries, keys, values):
    rows = queries.shape[0]
    z, _ = place_of()
    by_head = jnp.concatenate(
        [keys.reshape(rows, KVH, HD), values.reshape(rows, KVH, HD)], axis=2
    ).transpose(1, 0, 2)
    own = exchange(by_head).reshape(ROWS, 2 * HD)
    other = lax.ppermute(own, "ctx", Z_SWAP)
    x = exchange(queries.reshape(rows, KVH, GROUP * HD).transpose(1, 0, 2))
    x = x.reshape(ROWS, GROUP * HD)
    kv = jnp.concatenate(
        [jnp.where(z == 0, own, other), jnp.where(z == 0, other, own)], axis=0
    )
    got = {}
    got[1] = lax.ppermute(kv, "ctx", ring(1))
    got[-1] = lax.ppermute(kv, "ctx", ring(-1))
    state = own_block(x, kv)
    for step, shifts in ((1, (1,)), (2, (-1,)), (3, (2, -2, 3, -3))):
        got[step], state = lax.optimization_barrier((got[step], state))
        got[step + 1] = lax.ppermute(got[step], "ctx", ring(1))
        if step < NY // 2 - 1:
            got[-step - 1] = lax.ppermute(got[-step], "ctx", ring(-1))
        state = more_blocks([(at, got[at]) for at in shifts], x, state)
    out = last_blocks([(NY // 2, got[NY // 2])], x, state)
    out = exchange(out.reshape(NX, rows, GROUP * HD))
    return out.transpose(1, 0, 2).reshape(rows, QH * HD)


def solution(mesh):
    spec = P(("dp", "ctx"), None)
    return jax.shard_map(
        local, mesh=mesh, in_specs=(spec,) * 3, out_specs=spec, check_vma=False
    )
```

```python
import functools
import math

import jax
import jax.numpy as jnp
from jax import lax
from jax.experimental import pallas as pl
from jax.experimental.pallas import tpu as pltpu
from jax.sharding import PartitionSpec as P

QH = 32
KVH = 4
HD = 128
GROUP = QH // KVH
NZ, NY, NX = 2, 8, 4
ROWS = 256
SCALE = math.log2(math.e) / math.sqrt(HD)
NEG = -1e30
QK = (((1,), (1,)), ((), ()))


def index(z, y, x):
    return z * (NY * NX) + y * NX + x


X_GROUPS = [[index(z, y, x) for x in range(NX)] for z in range(NZ) for y in range(NY)]
Z_SWAP = [
    (index(z, y, x), index(1 - z, y, x))
    for z in range(NZ)
    for y in range(NY)
    for x in range(NX)
]


def place_of():
    me = lax.axis_index("ctx")
    return me // (NY * NX), lax.rem(me // NX, NY)


def exchange(pieces):
    return lax.all_to_all(
        pieces, "ctx", 0, 0, axis_index_groups=X_GROUPS, tiled=True
    )


def ring(direction, step, halves=(0, 1)):
    pairs = []
    for z in halves:
        for y in range(NY):
            origin = (y - direction * (step - 1)) % NY
            last = NY // 2 if direction == 1 else NY // 2 - 1
            reached = [(origin + direction * k) % NY for k in range(step, last + 1)]
            if z == 1 or any(origin < there for there in reached):
                target = (y + direction) % NY
                pairs += [(index(z, y, x), index(z, target, x)) for x in range(NX)]
    return pairs


def per_head(n, x_ref, key_scr, finish):
    def scores_of(j):
        return lax.dot_general(
            x_ref[:, j * HD : (j + 1) * HD],
            key_scr[:n, :],
            QK,
            preferred_element_type=jnp.float32,
        )

    scores = scores_of(0)
    for j in range(GROUP):
        ahead = scores_of(j + 1) if j + 1 < GROUP else None
        finish(slice(j * HD, (j + 1) * HD), scores)
        scores = ahead


def weigh(n, weights, value_scr):
    both = jnp.dot(
        weights.astype(jnp.bfloat16),
        value_scr[:n, :],
        preferred_element_type=jnp.float32,
    )
    return both[:, :HD], both[:, HD:]


def own_kernel(x_ref, kv_ref, acc_ref, max_ref, sum_ref, key_scr, value_scr):
    value_scr[:, HD:] = jnp.ones((2 * ROWS, HD), jnp.bfloat16)
    key_scr[...] = kv_ref[:, :HD]
    value_scr[:, :HD] = kv_ref[:, HD:]
    shape = (ROWS, 2 * ROWS)
    row = lax.broadcasted_iota(jnp.int32, shape, 0)
    col = lax.broadcasted_iota(jnp.int32, shape, 1)
    seen = col <= row + place_of()[0] * ROWS

    def finish(cols, scores):
        scores = jnp.where(seen, scores, NEG)
        peak = jnp.max(scores, axis=1, keepdims=True) * SCALE
        weights = jnp.exp2(scores * SCALE - peak)
        acc_ref[:, cols], sum_ref[:, cols] = weigh(2 * ROWS, weights, value_scr)
        max_ref[:, cols] = jnp.broadcast_to(peak, (ROWS, HD))

    per_head(2 * ROWS, x_ref, key_scr, finish)


def more_kernel(shifts, last, *refs):
    n = len(shifts)
    x_ref, firsts, seconds = refs[0], refs[1 : 1 + n], refs[1 + n : 1 + 2 * n]
    acc_in, max_in, sum_in = refs[1 + 2 * n : 4 + 2 * n]
    outs, (key_scr, value_scr) = refs[4 + 2 * n : -2], refs[-2:]
    z, y = place_of()
    before = [lax.rem(y - shift + NY, NY) < y for shift in shifts]

    def put(c, seen, key, value, safe):
        rows = slice(c * ROWS, (c + 1) * ROWS)
        zeros, ones = jnp.zeros_like(value), jnp.ones_like(value)
        key_scr[rows, :] = key if seen is None else jnp.where(seen, key, safe)
        value_scr[rows, :HD] = value if seen is None else jnp.where(seen, value, zeros)
        value_scr[rows, HD:] = ones if seen is None else jnp.where(seen, ones, zeros)

    def attend(keys):
        def finish(cols, scores):
            old = max_in[:, cols]
            peak = jnp.maximum(old, jnp.max(scores, axis=1, keepdims=True) * SCALE)
            keep = jnp.exp2(old - peak)
            weights = jnp.exp2(scores * SCALE - jnp.tile(peak, (1, keys // HD)))
            acc, total = weigh(keys, weights, value_scr)
            acc = acc_in[:, cols] * keep + acc
            total = sum_in[:, cols] * keep + total
            if last:
                outs[0][:, cols] = (acc / total).astype(jnp.bfloat16)
            else:
                outs[0][:, cols], outs[1][:, cols], outs[2][:, cols] = acc, peak, total

        per_head(keys, x_ref, key_scr, finish)

    @pl.when(z == 1)
    def _():
        for b in range(n):
            key = seconds[b][:ROWS, :HD]
            put(2 * b, None, key, seconds[b][:ROWS, HD:], None)
            put(2 * b + 1, before[b], seconds[b][ROWS:, :HD], seconds[b][ROWS:, HD:], key)
        attend(2 * ROWS * n)

    some = functools.reduce(jnp.logical_or, before)

    @pl.when(jnp.logical_and(z == 0, some))
    def _():
        safe = firsts[n - 1][:ROWS, :HD]
        for b in range(n - 2, -1, -1):
            safe = jnp.where(before[b], firsts[b][:ROWS, :HD], safe)
        for b in range(n):
            put(b, before[b], firsts[b][:ROWS, :HD], firsts[b][:ROWS, HD:], safe)
        attend(ROWS * n)

    if last:

        @pl.when(jnp.logical_and(z == 0, jnp.logical_not(some)))
        def _():
            outs[0][...] = (acc_in[...] / sum_in[...]).astype(jnp.bfloat16)


VMEM = pl.BlockSpec(memory_space=pltpu.VMEM)
STATE = [jax.ShapeDtypeStruct((ROWS, GROUP * HD), jnp.float32)] * 3
PARAMS = pltpu.CompilerParams(vmem_limit_bytes=32 << 20)


def cost(blocks):
    pairs = ROWS * GROUP * 2 * ROWS * blocks
    return pl.CostEstimate(
        flops=4 * pairs * HD, bytes_accessed=8 << 20, transcendentals=pairs
    )


def scratch(blocks):
    return [
        pltpu.VMEM((2 * ROWS * blocks, HD), jnp.bfloat16),
        pltpu.VMEM((2 * ROWS * blocks, 2 * HD), jnp.bfloat16),
    ]


def own_block(x, kv):
    return pl.pallas_call(
        own_kernel,
        out_shape=STATE,
        in_specs=[VMEM, VMEM],
        out_specs=[VMEM] * 3,
        scratch_shapes=scratch(1),
        compiler_params=PARAMS,
        cost_estimate=cost(1),
        name="own_block",
    )(x, kv)


def absorb(arrived, x, state, last=False):
    shifts, firsts, seconds = zip(*arrived)
    n = len(shifts)
    at = 1 + 2 * n
    out = [jax.ShapeDtypeStruct((ROWS, GROUP * HD), jnp.bfloat16)] if last else STATE
    return pl.pallas_call(
        functools.partial(more_kernel, shifts, last),
        out_shape=out,
        in_specs=[VMEM] * (2 * n + 4),
        out_specs=[VMEM] * len(out),
        scratch_shapes=scratch(n),
        input_output_aliases={} if last else {at: 0, at + 1: 1, at + 2: 2},
        compiler_params=PARAMS,
        cost_estimate=cost(n),
        name="last_blocks" if last else "more_blocks",
    )(x, *firsts, *seconds, *state)


def local(queries, keys, values):
    rows = queries.shape[0]
    z, _ = place_of()
    by_head = jnp.concatenate(
        [keys.reshape(rows, KVH, HD), values.reshape(rows, KVH, HD)], axis=2
    ).transpose(1, 0, 2)
    own = exchange(by_head).reshape(ROWS, 2 * HD)
    other = lax.ppermute(own, "ctx", Z_SWAP)
    x = exchange(queries.reshape(rows, KVH, GROUP * HD).transpose(1, 0, 2))
    x = x.reshape(ROWS, GROUP * HD)
    kv = jnp.concatenate(
        [jnp.where(z == 0, own, other), jnp.where(z == 0, other, own)], axis=0
    )
    got = {}
    got[1] = lax.ppermute(kv, "ctx", ring(1, 1))
    got[-1] = lax.ppermute(kv, "ctx", ring(-1, 1))
    state = own_block(x, kv)
    for step, shifts in ((1, (1,)), (2, (-1,)), (3, (2, -2, 3, -3))):
        got[step], state = lax.optimization_barrier((got[step], state))
        if step < NY // 2 - 1:
            got[step + 1] = lax.ppermute(got[step], "ctx", ring(1, step + 1))
            got[-step - 1] = lax.ppermute(got[-step], "ctx", ring(-1, step + 1))
        else:
            last = (
                step + 1,
                lax.ppermute(got[step][:ROWS], "ctx", ring(1, step + 1, (0,))),
                lax.ppermute(got[step], "ctx", ring(1, step + 1, (1,))),
            )
        state = absorb([(at, got[at], got[at]) for at in shifts], x, state)
    (out,) = absorb([last], x, state, last=True)
    out = exchange(out.reshape(NX, rows, GROUP * HD))
    return out.transpose(1, 0, 2).reshape(rows, QH * HD)


def solution(mesh):
    spec = P(("dp", "ctx"), None)
    return jax.shard_map(
        local, mesh=mesh, in_specs=(spec,) * 3, out_specs=spec, check_vma=False
    )
```

```python
import functools
import math

import jax
import jax.numpy as jnp
from jax import lax
from jax.experimental import pallas as pl
from jax.experimental.pallas import tpu as pltpu
from jax.sharding import PartitionSpec as P

QH = 32
KVH = 4
HD = 128
GROUP = QH // KVH
NZ, NY, NX = 2, 8, 4
ROWS = 256
SCALE = math.log2(math.e) / math.sqrt(HD)
NEG = -1e30
QK = (((1,), (1,)), ((), ()))


def index(z, y, x):
    return z * (NY * NX) + y * NX + x


X_GROUPS = [[index(z, y, x) for x in range(NX)] for z in range(NZ) for y in range(NY)]
Z_SWAP = [
    (index(z, y, x), index(1 - z, y, x))
    for z in range(NZ)
    for y in range(NY)
    for x in range(NX)
]


def place_of():
    me = lax.axis_index("ctx")
    return me // (NY * NX), lax.rem(me // NX, NY)


def exchange(pieces):
    return lax.all_to_all(
        pieces, "ctx", 0, 0, axis_index_groups=X_GROUPS, tiled=True
    )


def ring(direction, step, halves=(0, 1)):
    pairs = []
    for z in halves:
        for y in range(NY):
            origin = (y - direction * (step - 1)) % NY
            last = NY // 2 if direction == 1 else NY // 2 - 1
            reached = [(origin + direction * k) % NY for k in range(step, last + 1)]
            if z == 1 or any(origin < there for there in reached):
                target = (y + direction) % NY
                pairs += [(index(z, y, x), index(z, target, x)) for x in range(NX)]
    return pairs


def per_head(n, x_ref, key_scr, finish):
    def scores_of(j):
        return lax.dot_general(
            x_ref[:, j * HD : (j + 1) * HD],
            key_scr[:n, :],
            QK,
            preferred_element_type=jnp.float32,
        )

    scores = scores_of(0)
    for j in range(GROUP):
        ahead = scores_of(j + 1) if j + 1 < GROUP else None
        finish(slice(j * HD, (j + 1) * HD), scores)
        scores = ahead


def weigh(n, weights, value_scr):
    both = jnp.dot(
        weights.astype(jnp.bfloat16),
        value_scr[:n, :],
        preferred_element_type=jnp.float32,
    )
    return both[:, :HD], both[:, HD:]


def own_kernel(x_ref, kv_ref, acc_ref, max_ref, sum_ref, key_scr, value_scr):
    value_scr[:, HD:] = jnp.ones((2 * ROWS, HD), jnp.bfloat16)
    key_scr[...] = kv_ref[:, :HD]
    value_scr[:, :HD] = kv_ref[:, HD:]
    shape = (ROWS, 2 * ROWS)
    row = lax.broadcasted_iota(jnp.int32, shape, 0)
    col = lax.broadcasted_iota(jnp.int32, shape, 1)
    seen = col <= row + place_of()[0] * ROWS

    def finish(cols, scores):
        scores = jnp.where(seen, scores, NEG)
        peak = jnp.max(scores, axis=1, keepdims=True) * SCALE
        weights = jnp.exp2(scores * SCALE - peak)
        acc_ref[:, cols], sum_ref[:, cols] = weigh(2 * ROWS, weights, value_scr)
        max_ref[:, cols] = jnp.broadcast_to(peak, (ROWS, HD))

    per_head(2 * ROWS, x_ref, key_scr, finish)


def more_kernel(shifts, last, *refs):
    n = len(shifts)
    x_ref, firsts, seconds = refs[0], refs[1 : 1 + n], refs[1 + n : 1 + 2 * n]
    acc_in, max_in, sum_in = refs[1 + 2 * n : 4 + 2 * n]
    outs, (key_scr, value_scr) = refs[4 + 2 * n : -2], refs[-2:]
    z, y = place_of()
    before = [lax.rem(y - shift + NY, NY) < y for shift in shifts]

    def put(c, seen, key, value, safe):
        rows = slice(c * ROWS, (c + 1) * ROWS)
        zeros, ones = jnp.zeros_like(value), jnp.ones_like(value)
        key_scr[rows, :] = key if seen is None else jnp.where(seen, key, safe)
        value_scr[rows, :HD] = value if seen is None else jnp.where(seen, value, zeros)
        value_scr[rows, HD:] = ones if seen is None else jnp.where(seen, ones, zeros)

    def attend(keys):
        def finish(cols, scores):
            old = max_in[:, cols]
            peak = jnp.maximum(old, jnp.max(scores, axis=1, keepdims=True) * SCALE)
            keep = jnp.exp2(old - peak)
            weights = jnp.exp2(scores * SCALE - jnp.tile(peak, (1, keys // HD)))
            acc, total = weigh(keys, weights, value_scr)
            acc = acc_in[:, cols] * keep + acc
            total = sum_in[:, cols] * keep + total
            if last:
                outs[0][:, cols] = (acc / total).astype(jnp.bfloat16)
            else:
                outs[0][:, cols], outs[1][:, cols], outs[2][:, cols] = acc, peak, total

        per_head(keys, x_ref, key_scr, finish)

    @pl.when(z == 1)
    def _():
        for b in range(n):
            key = seconds[b][:ROWS, :HD]
            put(2 * b, None, key, seconds[b][:ROWS, HD:], None)
            put(2 * b + 1, before[b], seconds[b][ROWS:, :HD], seconds[b][ROWS:, HD:], key)
        attend(2 * ROWS * n)

    some = functools.reduce(jnp.logical_or, before)

    @pl.when(jnp.logical_and(z == 0, some))
    def _():
        safe = firsts[n - 1][:ROWS, :HD]
        for b in range(n - 2, -1, -1):
            safe = jnp.where(before[b], firsts[b][:ROWS, :HD], safe)
        for b in range(n):
            put(b, before[b], firsts[b][:ROWS, :HD], firsts[b][:ROWS, HD:], safe)
        attend(ROWS * n)

    if last:

        @pl.when(jnp.logical_and(z == 0, jnp.logical_not(some)))
        def _():
            outs[0][...] = (acc_in[...] / sum_in[...]).astype(jnp.bfloat16)


VMEM = pl.BlockSpec(memory_space=pltpu.VMEM)
STATE = [jax.ShapeDtypeStruct((ROWS, GROUP * HD), jnp.float32)] * 3
PARAMS = pltpu.CompilerParams(vmem_limit_bytes=32 << 20)


def cost(blocks):
    pairs = ROWS * GROUP * 2 * ROWS * blocks
    return pl.CostEstimate(
        flops=4 * pairs * HD, bytes_accessed=8 << 20, transcendentals=pairs
    )


def scratch(blocks):
    return [
        pltpu.VMEM((2 * ROWS * blocks, HD), jnp.bfloat16),
        pltpu.VMEM((2 * ROWS * blocks, 2 * HD), jnp.bfloat16),
    ]


def own_block(x, kv):
    return pl.pallas_call(
        own_kernel,
        out_shape=STATE,
        in_specs=[VMEM, VMEM],
        out_specs=[VMEM] * 3,
        scratch_shapes=scratch(1),
        compiler_params=PARAMS,
        cost_estimate=cost(1),
        name="own_block",
    )(x, kv)


def absorb(arrived, x, state, last=False):
    shifts, firsts, seconds = zip(*arrived)
    n = len(shifts)
    at = 1 + 2 * n
    out = [jax.ShapeDtypeStruct((ROWS, GROUP * HD), jnp.bfloat16)] if last else STATE
    return pl.pallas_call(
        functools.partial(more_kernel, shifts, last),
        out_shape=out,
        in_specs=[VMEM] * (2 * n + 4),
        out_specs=[VMEM] * len(out),
        scratch_shapes=scratch(n),
        input_output_aliases={} if last else {at: 0, at + 1: 1, at + 2: 2},
        compiler_params=PARAMS,
        cost_estimate=cost(n),
        name="last_blocks" if last else "more_blocks",
    )(x, *firsts, *seconds, *state)


def local(queries, keys, values):
    rows = queries.shape[0]
    z, _ = place_of()
    by_head = jnp.concatenate(
        [keys.reshape(rows, KVH, HD), values.reshape(rows, KVH, HD)], axis=2
    ).transpose(1, 0, 2)
    own = exchange(by_head).reshape(ROWS, 2 * HD)
    other = lax.ppermute(own, "ctx", Z_SWAP)
    x = exchange(queries.reshape(rows, KVH, GROUP * HD).transpose(1, 0, 2))
    x = x.reshape(ROWS, GROUP * HD)
    kv = jnp.concatenate(
        [jnp.where(z == 0, own, other), jnp.where(z == 0, other, own)], axis=0
    )
    def send_up(first, second, step):
        return (
            lax.ppermute(first, "ctx", ring(1, step, (0,))),
            lax.ppermute(second, "ctx", ring(1, step, (1,))),
        )

    got = {1: send_up(kv[:ROWS], kv, 1)}
    down = lax.ppermute(kv, "ctx", ring(-1, 1))
    got[-1] = (down, down)
    state = own_block(x, kv)
    for step, shifts in ((1, (1,)), (2, (-1,)), (3, (2, -2, 3, -3))):
        up, state = lax.optimization_barrier((got[step], state))
        got[step] = up
        got[step + 1] = send_up(*up, step + 1)
        if step < NY // 2 - 1:
            down = lax.ppermute(down, "ctx", ring(-1, step + 1))
            got[-step - 1] = (down, down)
        state = absorb([(at, *got[at]) for at in shifts], x, state)
    (out,) = absorb([(NY // 2, *got[NY // 2])], x, state, last=True)
    out = exchange(out.reshape(NX, rows, GROUP * HD))
    return out.transpose(1, 0, 2).reshape(rows, QH * HD)


def solution(mesh):
    spec = P(("dp", "ctx"), None)
    return jax.shard_map(
        local, mesh=mesh, in_specs=(spec,) * 3, out_specs=spec, check_vma=False
    )
```

```python
import functools
import math

import jax
import jax.numpy as jnp
from jax import lax
from jax.experimental import pallas as pl
from jax.experimental.pallas import tpu as pltpu
from jax.sharding import PartitionSpec as P


QH = 32
KVH = 4
HD = 128
GROUP = QH // KVH
NZ, NY, NX = 2, 8, 4
ROWS = 256
SCALE = math.log2(math.e) / math.sqrt(HD)
NEG = -1e30
QK = (((1,), (1,)), ((), ()))


def index(z, y, x):
    return z * (NY * NX) + y * NX + x


X_GROUPS = [[index(z, y, x) for x in range(NX)] for z in range(NZ) for y in range(NY)]
Z_SWAP = [
    (index(z, y, x), index(1 - z, y, x))
    for z in range(NZ)
    for y in range(NY)
    for x in range(NX)
]


def place_of():
    me = lax.axis_index("ctx")
    return me // (NY * NX), lax.rem(me // NX, NY)


def exchange(pieces):
    return lax.all_to_all(
        pieces, "ctx", 0, 0, axis_index_groups=X_GROUPS, tiled=True
    )


def ring(direction, step, halves=(0, 1)):
    pairs = []
    for z in halves:
        for y in range(NY):
            origin = (y - direction * (step - 1)) % NY
            last = NY // 2 if direction == 1 else NY // 2 - 1
            reached = [(origin + direction * k) % NY for k in range(step, last + 1)]
            if z == 1 or any(origin < there for there in reached):
                target = (y + direction) % NY
                pairs += [(index(z, y, x), index(z, target, x)) for x in range(NX)]
    return pairs


def per_head(n, x_ref, key_scr, finish):
    def scores_of(j):
        return lax.dot_general(
            x_ref[:, j * HD : (j + 1) * HD],
            key_scr[:n, :],
            QK,
            preferred_element_type=jnp.float32,
        )

    scores = scores_of(0)
    for j in range(GROUP):
        ahead = scores_of(j + 1) if j + 1 < GROUP else None
        finish(slice(j * HD, (j + 1) * HD), scores)
        scores = ahead


def weigh(n, weights, value_scr):
    both = jnp.dot(
        weights.astype(jnp.bfloat16),
        value_scr[:n, :],
        preferred_element_type=jnp.float32,
    )
    return both[:, :HD], both[:, HD:]


def own_kernel(x_ref, kv_ref, acc_ref, max_ref, sum_ref, key_scr, value_scr):
    value_scr[:, HD:] = jnp.ones((2 * ROWS, HD), jnp.bfloat16)
    key_scr[...] = kv_ref[:, :HD]
    value_scr[:, :HD] = kv_ref[:, HD:]
    shape = (ROWS, 2 * ROWS)
    row = lax.broadcasted_iota(jnp.int32, shape, 0)
    col = lax.broadcasted_iota(jnp.int32, shape, 1)
    seen = col <= row + place_of()[0] * ROWS

    def finish(cols, scores):
        scores = jnp.where(seen, scores, NEG)
        peak = jnp.max(scores, axis=1, keepdims=True) * SCALE
        weights = jnp.exp2(scores * SCALE - peak)
        acc_ref[:, cols], sum_ref[:, cols] = weigh(2 * ROWS, weights, value_scr)
        max_ref[:, cols] = jnp.broadcast_to(peak, (ROWS, HD))

    per_head(2 * ROWS, x_ref, key_scr, finish)


def more_kernel(shifts, last, *refs):
    n = len(shifts)
    x_ref, firsts, seconds = refs[0], refs[1 : 1 + n], refs[1 + n : 1 + 2 * n]
    acc_in, max_in, sum_in = refs[1 + 2 * n : 4 + 2 * n]
    outs, (key_scr, value_scr) = refs[4 + 2 * n : -2], refs[-2:]
    z, y = place_of()
    before = [lax.rem(y - shift + NY, NY) < y for shift in shifts]

    def put(c, seen, key, value, safe):
        rows = slice(c * ROWS, (c + 1) * ROWS)
        zeros, ones = jnp.zeros_like(value), jnp.ones_like(value)
        key_scr[rows, :] = key if seen is None else jnp.where(seen, key, safe)
        value_scr[rows, :HD] = value if seen is None else jnp.where(seen, value, zeros)
        value_scr[rows, HD:] = ones if seen is None else jnp.where(seen, ones, zeros)

    def attend(keys):
        def finish(cols, scores):
            old = max_in[:, cols]
            peak = jnp.maximum(old, jnp.max(scores, axis=1, keepdims=True) * SCALE)
            keep = jnp.exp2(old - peak)
            weights = jnp.exp2(scores * SCALE - jnp.tile(peak, (1, keys // HD)))
            acc, total = weigh(keys, weights, value_scr)
            acc = acc_in[:, cols] * keep + acc
            total = sum_in[:, cols] * keep + total
            if last:
                outs[0][:, cols] = (acc / total).astype(jnp.bfloat16)
            else:
                outs[0][:, cols], outs[1][:, cols], outs[2][:, cols] = acc, peak, total

        per_head(keys, x_ref, key_scr, finish)

    @pl.when(z == 1)
    def _():
        for b in range(n):
            key = seconds[b][:ROWS, :HD]
            put(2 * b, None, key, seconds[b][:ROWS, HD:], None)
            put(2 * b + 1, before[b], seconds[b][ROWS:, :HD], seconds[b][ROWS:, HD:], key)
        attend(2 * ROWS * n)

    some = functools.reduce(jnp.logical_or, before)

    @pl.when(jnp.logical_and(z == 0, some))
    def _():
        safe = firsts[n - 1][:ROWS, :HD]
        for b in range(n - 2, -1, -1):
            safe = jnp.where(before[b], firsts[b][:ROWS, :HD], safe)
        for b in range(n):
            put(b, before[b], firsts[b][:ROWS, :HD], firsts[b][:ROWS, HD:], safe)
        attend(ROWS * n)

    if last:

        @pl.when(jnp.logical_and(z == 0, jnp.logical_not(some)))
        def _():
            outs[0][...] = (acc_in[...] / sum_in[...]).astype(jnp.bfloat16)


VMEM = pl.BlockSpec(memory_space=pltpu.VMEM)
STATE = [jax.ShapeDtypeStruct((ROWS, GROUP * HD), jnp.float32)] * 3
PARAMS = pltpu.CompilerParams(vmem_limit_bytes=32 << 20)


def cost(blocks):
    pairs = ROWS * GROUP * 2 * ROWS * blocks
    return pl.CostEstimate(
        flops=4 * pairs * HD, bytes_accessed=8 << 20, transcendentals=pairs
    )


def scratch(blocks):
    return [
        pltpu.VMEM((2 * ROWS * blocks, HD), jnp.bfloat16),
        pltpu.VMEM((2 * ROWS * blocks, 2 * HD), jnp.bfloat16),
    ]


def own_block(x, kv):
    return pl.pallas_call(
        own_kernel,
        out_shape=STATE,
        in_specs=[VMEM, VMEM],
        out_specs=[VMEM] * 3,
        scratch_shapes=scratch(1),
        compiler_params=PARAMS,
        cost_estimate=cost(1),
        name="own_block",
    )(x, kv)


def absorb(arrived, x, state, last=False):
    shifts, firsts, seconds = zip(*arrived)
    n = len(shifts)
    at = 1 + 2 * n
    out = [jax.ShapeDtypeStruct((ROWS, GROUP * HD), jnp.bfloat16)] if last else STATE
    return pl.pallas_call(
        functools.partial(more_kernel, shifts, last),
        out_shape=out,
        in_specs=[VMEM] * (2 * n + 4),
        out_specs=[VMEM] * len(out),
        scratch_shapes=scratch(n),
        input_output_aliases={} if last else {at: 0, at + 1: 1, at + 2: 2},
        compiler_params=PARAMS,
        cost_estimate=cost(n),
        name="last_blocks" if last else "more_blocks",
    )(x, *firsts, *seconds, *state)


def attention(queries, keys, values):
    rows = queries.shape[0]
    z, _ = place_of()
    by_head = jnp.concatenate(
        [keys.reshape(rows, KVH, HD), values.reshape(rows, KVH, HD)], axis=2
    ).transpose(1, 0, 2)
    own = exchange(by_head).reshape(ROWS, 2 * HD)
    other = lax.ppermute(own, "ctx", Z_SWAP)
    x = exchange(queries.reshape(rows, KVH, GROUP * HD).transpose(1, 0, 2))
    x = x.reshape(ROWS, GROUP * HD)
    kv = jnp.concatenate(
        [jnp.where(z == 0, own, other), jnp.where(z == 0, other, own)], axis=0
    )

    def send_up(first, second, step):
        first = lax.ppermute(first, "ctx", ring(1, step, (0,)))
        second = lax.ppermute(second, "ctx", ring(1, step, (1,)))
        return first, second

    got = {1: send_up(kv[:ROWS], kv, 1)}
    down = lax.ppermute(kv, "ctx", ring(-1, 1))
    got[-1] = (down, down)
    state = own_block(x, kv)
    for step, shifts in ((1, (1,)), (2, (-1,)), (3, (2, -2, 3, -3))):
        up, state = lax.optimization_barrier((got[step], state))
        got[step] = up
        got[step + 1] = send_up(*up, step + 1)
        if step < NY // 2 - 1:
            down = lax.ppermute(down, "ctx", ring(-1, step + 1))
            got[-step - 1] = (down, down)
        state = absorb([(at, *got[at]) for at in shifts], x, state)
    (out,) = absorb([(NY // 2, *got[NY // 2])], x, state, last=True)
    out = exchange(out.reshape(NX, rows, GROUP * HD))
    return out.transpose(1, 0, 2).reshape(rows, QH * HD)


def solution(mesh):
    spec = P(("dp", "ctx"), None)
    return jax.shard_map(
        attention, mesh=mesh, in_specs=(spec,) * 3, out_specs=spec, check_vma=False
    )
```
